512 devices in a mesh: ctx: 64 (over z, x), head: 8 (over y, core).
Axes of the slice: x: 4, y: 4, z: 16, core: 2. Of those that a mesh axis runs over, the one named last changes fastest.
Arguments:
- q_ret: bfloat16 [8192, 4096], P('ctx', 'head'), may hold values from -6 to 6
- k_ret: bfloat16 [8192, 4096], P('ctx', 'head'), may hold values from -6 to 6
- v_ret: bfloat16 [8192, 4096], P('ctx', 'head'), may hold values from -6 to 6
- gate_ret: bfloat16 [8192, 4096], P('ctx', 'head'), may hold values from -6 to 6
- log_decay: float32 [8192, 16], P('ctx', 'head'), may hold values from -2 to 0
- q_cross: bfloat16 [8192, 4096], P('ctx', 'head'), may hold values from -32 to 32
- cache_k: bfloat16 [8192, 2048], P(('ctx', 'head')), may hold values from -16 to 16
- cache_v: bfloat16 [8192, 2048], P(('ctx', 'head')), may hold values from -6 to 6
Outputs:
- o_ret: bfloat16 [8192, 4096], P('ctx', 'head')
- o_cross: bfloat16 [8192, 4096], P('ctx', 'head')
The draws below stay inside these ranges and needn't reach their ends.
All inputs are finite; a program needn't handle non-finite values.
Results may differ from the reference program's by a relative error of at most 0.0039.
Values may be sent and summed in bfloat16 or wider, within the bound.
A program may use at most 128 MiB of HBM per device.

```python
import math
import jax
import jax.numpy as jnp
from jax import lax

TOK_DEV = 128
HD = 256
RETENTION_HEADS = 16
CACHE_HEADS = 8
PROMPT_TOKENS = 8192


def draw_q_cross(key, part):
    drawn_base = jnp.clip(2.5 * jax.random.normal(jax.random.fold_in(key, 1), (PROMPT_TOKENS, RETENTION_HEADS * HD), jnp.float32), -15.0, 15.0)
    return drawn_base.astype(jnp.bfloat16)


def draw_cache_k(key, part):
    drawn_base = jnp.clip(jax.random.normal(jax.random.fold_in(key, 2), (PROMPT_TOKENS, CACHE_HEADS * HD), jnp.float32), -6.0, 6.0)
    return drawn_base.astype(jnp.bfloat16)


def draw_log_decay(key, part):
    fast_count = 8
    quick_heads = jax.random.randint(jax.random.fold_in(key, 21), (RETENTION_HEADS,), 0, 16) < fast_count
    fast_rate = jnp.exp(jax.random.uniform(jax.random.fold_in(key, 22), (RETENTION_HEADS,), jnp.float32, math.log(3.0 / TOK_DEV), math.log(4.0 / TOK_DEV)))
    slow_rate = jnp.exp(jax.random.uniform(jax.random.fold_in(key, 23), (RETENTION_HEADS,), jnp.float32, math.log(1.0 / (64.0 * PROMPT_TOKENS)), math.log(1.0 / (8.0 * PROMPT_TOKENS))))
    head_rate = jnp.where(quick_heads, fast_rate, slow_rate)
    block_count = PROMPT_TOKENS // TOK_DEV
    block_factor = jnp.exp(jax.random.uniform(jax.random.fold_in(key, 24), (block_count, RETENTION_HEADS), jnp.float32, math.log(0.5), math.log(2.0)))
    block_factor = jnp.repeat(block_factor, TOK_DEV, axis=0)
    row_factor = jnp.exp(jax.random.uniform(jax.random.fold_in(key, 25), (PROMPT_TOKENS, RETENTION_HEADS), jnp.float32, math.log(0.5), math.log(2.0)))
    value_matrix = -head_rate[None, :] * block_factor * row_factor
    group_rows = jax.random.randint(jax.random.fold_in(key, 26), (2,), 0, PROMPT_TOKENS)
    group_length = jax.random.uniform(jax.random.fold_in(key, 27), (2, RETENTION_HEADS), jnp.float32, math.log(0.5), math.log(0.8))
    value_matrix = value_matrix.at[group_rows].add(group_length)
    return value_matrix


def steps_of(rng, dims, cuts, least, top_value):
    loudness, own = 1.0, jax.random.fold_in(rng, 6)
    for dim, parts in cuts:
        draws = jnp.exp(jax.random.uniform(jax.random.fold_in(own, dim), (parts,), jnp.float32, least / len(cuts), top_value / len(cuts)))
        loudness = loudness * jnp.repeat(draws, dims[dim] // parts).reshape([-1 if axis == dim else 1 for axis in range(len(dims))])
    return loudness


def bell_draw(rng, dims, scale, bound, split=(), held_as=jnp.bfloat16):
    result = jax.random.normal(rng, dims, jnp.float32) * scale
    if len(split) > 0:
        result = steps_of(rng, dims, split, -0.22, 0.18) * result
    return jnp.clip(result, min=-bound, max=bound).astype(held_as)


def setup_inputs(seed: int = 0) -> dict:
    key_of = jax.random.split(jax.random.key(seed), 9)
    q_ret = bell_draw(key_of[0], (PROMPT_TOKENS, RETENTION_HEADS * HD), 1.0, 6.0, ((0, 64), (1, 8)))
    k_ret = bell_draw(key_of[1], (PROMPT_TOKENS, RETENTION_HEADS * HD), 1.0, 6.0, ((0, 64), (1, 8)))
    v_ret = bell_draw(key_of[2], (PROMPT_TOKENS, RETENTION_HEADS * HD), 1.0, 6.0, ((0, 64), (1, 8)))
    gate_ret = bell_draw(key_of[3], (PROMPT_TOKENS, RETENTION_HEADS * HD), 1.0, 6.0, ((0, 64), (1, 8)))
    log_decay = draw_log_decay(jax.random.fold_in(key_of[8], 71), 0)
    q_cross = draw_q_cross(jax.random.fold_in(key_of[8], 71), 0)
    cache_k = draw_cache_k(jax.random.fold_in(key_of[8], 71), 0)
    cache_v = bell_draw(key_of[7], (PROMPT_TOKENS, CACHE_HEADS * HD), 1.0, 6.0, ((0, 512),))
    return {"q_ret": q_ret, "k_ret": k_ret, "v_ret": v_ret, "gate_ret": gate_ret, "log_decay": log_decay, "q_cross": q_cross, "cache_k": cache_k, "cache_v": cache_v}


norm_eps = 1e-06
highest = lax.Precision.HIGHEST

def by_heads(matrix_in):
    return matrix_in.reshape(matrix_in.shape[0], matrix_in.shape[1] // HD, HD).transpose(1, 0, 2)

def from_heads(stacked):
    return stacked.transpose(1, 0, 2).reshape(stacked.shape[1], stacked.shape[0] * HD)

def retention_all(q_ret, k_ret, v_ret, gate_ret, log_decay):
    span_len = TOK_DEV
    blocks = PROMPT_TOKENS // span_len

    def to_blocks(matrix_in):
        heads_first = by_heads(matrix_in)
        return heads_first.reshape(RETENTION_HEADS, blocks, span_len, HD).transpose(1, 0, 2, 3)
    queries = to_blocks(q_ret)
    key_heads = to_blocks(k_ret)
    value_heads = to_blocks(v_ret)
    decay_blocks = log_decay.reshape(blocks, span_len, RETENTION_HEADS)
    position = jnp.arange(span_len, dtype=jnp.int32)
    causal = position[:, None] >= position[None, :]

    def doubling_step(state_now, inputs):
        query_b, key_b, value_b, decay_b = inputs
        decay_sum = jnp.cumsum(decay_b, axis=0).T
        scores = jnp.einsum('hrd,hsd->hrs', query_b, key_b, preferred_element_type=jnp.float32)
        spread = jnp.minimum(decay_sum[:, :, None] - decay_sum[:, None, :], 0.0)
        weight_matrix = jnp.where(causal[None], jnp.exp(spread) * scores, 0.0).astype(jnp.bfloat16)
        within_block = jnp.einsum('hrs,hsd->hrd', weight_matrix, value_b, preferred_element_type=jnp.float32)
        from_before = jnp.exp(decay_sum)[:, :, None] * jnp.einsum('hrd,hde->hre', query_b.astype(jnp.float32), state_now, precision=highest)
        final_sum = decay_sum[:, -1]
        carried = (key_b.astype(jnp.float32) * jnp.exp(final_sum[:, None] - decay_sum)[:, :, None]).astype(jnp.bfloat16)
        summary = jnp.einsum('hsd,hse->hde', carried, value_b, preferred_element_type=jnp.float32)
        new_state = jnp.exp(final_sum)[:, None, None] * state_now + summary
        return (new_state, within_block + from_before)
    initial = jnp.zeros((RETENTION_HEADS, HD, HD), jnp.float32)
    unused, retained = lax.scan(doubling_step, initial, (queries, key_heads, value_heads, decay_blocks))
    retained = retained.transpose(1, 0, 2, 3).reshape(RETENTION_HEADS, PROMPT_TOKENS, HD)
    normed = retained * lax.rsqrt(lax.optimization_barrier(jnp.mean(retained * retained, axis=2, keepdims=True)) + norm_eps)
    gated_out = normed * jax.nn.silu(by_heads(gate_ret).astype(jnp.float32))
    return from_heads(gated_out).astype(jnp.bfloat16)

def cross_all(q_cross, cache_k, cache_v):
    span_len = math.gcd(PROMPT_TOKENS, 512)
    group_size = RETENTION_HEADS // CACHE_HEADS
    score_scale = 1.0 / math.sqrt(HD)
    queries = by_heads(q_cross)
    key_heads = jnp.repeat(by_heads(cache_k), group_size, axis=0)
    value_heads = jnp.repeat(by_heads(cache_v), group_size, axis=0)

    def one_head(inputs):
        query_h, key_h, value_h = inputs
        pieces = []
        for first_row in range(0, PROMPT_TOKENS, span_len):
            end_row = first_row + span_len
            scores = jnp.dot(query_h[first_row:end_row], key_h[:end_row].T, preferred_element_type=jnp.float32) * score_scale
            row_position = jnp.arange(first_row, end_row, dtype=jnp.int32)
            key_position = jnp.arange(0, end_row, dtype=jnp.int32)
            allowed = row_position[:, None] >= key_position[None, :]
            masked = jnp.where(allowed, scores, -jnp.inf)
            top_score = lax.optimization_barrier(jnp.max(masked, axis=1, keepdims=True))
            weight_matrix = jnp.where(allowed, jnp.exp(masked - top_score), 0.0)
            run_total = lax.optimization_barrier(jnp.sum(weight_matrix, axis=1, keepdims=True))
            mixed_out = jnp.dot(weight_matrix.astype(jnp.bfloat16), value_h[:end_row], preferred_element_type=jnp.float32)
            pieces.append(mixed_out / run_total)
        return jnp.concatenate(pieces, axis=0)
    stacked = lax.map(one_head, (queries, key_heads, value_heads))
    return from_heads(stacked).astype(jnp.bfloat16)

def reference(q_ret, k_ret, v_ret, gate_ret, log_decay, q_cross, cache_k, cache_v):
    o_ret = retention_all(q_ret, k_ret, v_ret, gate_ret, log_decay)
    o_cross = cross_all(q_cross, cache_k, cache_v)
    return (o_ret, o_cross)
```

```python
import functools
import math

import jax
import jax.numpy as jnp
from jax import lax
from jax.experimental import pallas as pl
from jax.experimental.pallas import tpu as pltpu
from jax.sharding import PartitionSpec as P

HD = 256
X = 4
NEG = -1e30
EPS = 1e-06
MESH = pl.DeviceIdType.MESH
bf16, f32 = jnp.bfloat16, jnp.float32
SCALE2 = math.log2(math.e) / math.sqrt(HD)
NT = (((1,), (1,)), ((), ()))
TN = (((0,), (0,)), ((), ()))


def mm(a, b, dims=(((1,), (0,)), ((), ()))):
    return lax.dot_general(a, b, dims, preferred_element_type=f32)


def wide(a):
    return jnp.concatenate([a, a], axis=1)


def kernel(
    Z, NH, T,
    q_ret, k_ret, v_ret, gate, ld, q_x, cache_k, cache_v,
    o_ret, o_x,
    qbuf, own, kv, gown, gbuf, m_s, l_s, acc, o_send, o_recv, st_send, st_recv,
    d_s, within, silu, sum_send, sum_recv, t_send, t_recv, qr, s_f, s_b, e_f,
    fb_send, fb_recv,
    loc_sem, c_send, c_recv, x_send, x_recv, z_send, z_recv,
):
    F = Z // 2
    B = F - 1
    RP = T // NH
    c = lax.axis_index("ctx")
    h = lax.axis_index("head")
    z = lax.div(c, X)
    x = lax.rem(c, X)
    plane = z * X

    def xdev(r):
        xp = lax.rem(x + r, X)
        return xp, (plane + xp, h)

    def hdev(r):
        hp = lax.rem(h + r, NH)
        return hp, (c, hp)

    up = (lax.rem(c + X, Z * X), h)
    down = (lax.rem(c + (Z - 1) * X, Z * X), h)

    def remote(src, dst, ss, rs, dev):
        return pltpu.make_async_remote_copy(
            src_ref=src, dst_ref=dst, send_sem=ss, recv_sem=rs,
            device_id=dev, device_id_type=MESH,
        )

    barrier = pltpu.get_barrier_semaphore()
    for r in range(1, NH):
        pl.semaphore_signal(barrier, inc=1, device_id=hdev(r)[1], device_id_type=MESH)
    for r in range(1, X):
        pl.semaphore_signal(barrier, inc=1, device_id=xdev(r)[1], device_id_type=MESH)
    pl.semaphore_signal(barrier, inc=1, device_id=up, device_id_type=MESH)
    pl.semaphore_signal(barrier, inc=1, device_id=down, device_id_type=MESH)

    def head_cols(i):
        return pl.ds(pl.multiple_of(i * HD, HD), HD)

    locals_ = [
        pltpu.make_async_copy(cache_k.at[:, head_cols(h)], own.at[0, pl.ds(pl.multiple_of(h * RP, RP), RP)], loc_sem.at[0]),
        pltpu.make_async_copy(cache_v.at[:, head_cols(h)], own.at[1, pl.ds(pl.multiple_of(h * RP, RP), RP)], loc_sem.at[1]),
        pltpu.make_async_copy(q_x.at[:, 0:HD], qbuf.at[x, 0], loc_sem.at[2]),
        pltpu.make_async_copy(q_x.at[:, HD:2 * HD], qbuf.at[x, 1], loc_sem.at[3]),
        pltpu.make_async_copy(q_ret.at[:, head_cols(lax.div(x, 2))], qr.at[x], loc_sem.at[4]),
    ]
    for cp in locals_:
        cp.start()

    rows = lax.broadcasted_iota(jnp.int32, (T, T), 0)
    cols = lax.broadcasted_iota(jnp.int32, (T, T), 1)
    for hh in range(2):
        d = jnp.broadcast_to(ld[:, hh:hh + 1], (T, T))
        step = 1
        while step < T:
            d = d + jnp.where(rows >= step, pltpu.roll(d, step, 0), 0.0)
            step *= 2
        d_s[hh] = d
        last = d[T - 1:T, :]
        fade = jnp.exp(last - d)
        kh = k_ret[:, hh * HD:(hh + 1) * HD]
        vh = v_ret[:, hh * HD:(hh + 1) * HD]
        carried = (kh.astype(f32) * wide(fade)).astype(bf16)
        summ = mm(carried, vh, TN)
        sum_send[2 * hh] = summ[:, :HD // 2]
        sum_send[2 * hh + 1] = summ[:, HD // 2:]
        t_send[4 * hh:4 * hh + 4, :] = jnp.broadcast_to(last, (4, T))

    pl.semaphore_wait(barrier, (NH - 1) + (X - 1) + 2)

    def cache_copy(r, t):
        src = cache_k if t == 0 else cache_v
        hp, dev = hdev(r)
        return remote(
            src.at[:, head_cols(hp)], own.at[t, pl.ds(pl.multiple_of(h * RP, RP), RP)],
            c_send.at[t, r], c_recv.at[t, r], dev,
        )

    for r in range(1, NH):
        for t in range(2):
            cache_copy(r, t).start()

    def x_copy(kind, r):
        xp, dev = xdev(r)
        if kind == 0:
            src, dst = sum_send.at[xp], sum_recv.at[x]
        elif kind == 1:
            src, dst = t_send, t_recv.at[x]
        elif kind == 2 or kind == 3:
            src, dst = q_x.at[:, (kind - 2) * HD:(kind - 1) * HD], qbuf.at[x, kind - 2]
        elif kind == 4:
            src, dst = q_ret.at[:, head_cols(lax.div(xp, 2))], qr.at[x]
        elif kind == 5:
            src, dst = o_send.at[xp], o_recv.at[x]
        elif kind == 6:
            src, dst = st_send.at[xp], st_recv.at[x]
        else:
            src, dst = fb_send.at[xp], fb_recv.at[x]
        return remote(src, dst, x_send.at[kind, r], x_recv.at[kind, r], dev)

    order = (2, 1, 3)
    for kind in (1, 0, 2, 3, 4):
        for r in order:
            x_copy(kind, r).start()

    sum_recv[x] = sum_send[x]
    t_recv[x] = t_send[...]
    for hh in range(2):
        d = d_s[hh]
        qh = q_ret[:, hh * HD:(hh + 1) * HD]
        kh = k_ret[:, hh * HD:(hh + 1) * HD]
        vh = v_ret[:, hh * HD:(hh + 1) * HD]
        spread = jnp.minimum(d - d.T, 0.0)
        w = jnp.where(rows >= cols, jnp.exp(spread) * mm(qh, kh, NT), 0.0).astype(bf16)
        within[hh] = mm(w, vh)
        g = gate[:, hh * HD:(hh + 1) * HD].astype(f32)
        silu[hh] = g / (1.0 + jnp.exp(-g))

    def slot(t, way, i):
        return gbuf.at[way, i] if t == 2 else kv.at[t, way, i]

    def mine(t):
        return gown if t == 2 else own.at[t]

    def send_own(t, way):
        return remote(mine(t), slot(t, way, 0), z_send.at[t, way, 0], z_recv.at[t, way, 0], up if way == 0 else down)

    back_shift = jnp.where(z < F, 1, 0)

    def pass_on(t, way, i):
        to = i + 1 if way == 0 else i + back_shift
        return remote(slot(t, way, i), slot(t, way, to), z_send.at[t, way, i + 1], z_recv.at[t, way, to], up if way == 0 else down)

    own_up = z < Z - 1
    own_down = z < B
    got_up = jnp.minimum(z, F)
    got_down = jnp.where(z < F, jnp.maximum(B - 1 - z, 0), z - F)
    use_down = jnp.where(z < F, 0, z - F)
    pass_up = jnp.where(z < Z - 1, jnp.minimum(z, F - 1), 0)
    pass_down = jnp.where(z < F, got_down, jnp.maximum(z - F - 1, 0))

    def start_own(t):
        @pl.when(own_up)
        def _():
            send_own(t, 0).start()

        @pl.when(own_down)
        def _():
            send_own(t, 1).start()

    locals_[0].wait()
    locals_[1].wait()
    for t in range(2):
        for r in range(1, NH):
            cache_copy(r, t).wait_recv()
        start_own(t)

    for kind in (1, 0):
        for r in order:
            x_copy(kind, (X - r) % X).wait_recv()

    second = lax.div(x, 2) == 1

    def total(i):
        tr = t_recv[i]
        return jnp.where(second, tr[4:5, :], tr[0:1, :])

    g = sum_recv[0]
    plane_sum = total(0)
    for i in range(1, X):
        g = g * jnp.exp(total(i)) + sum_recv[i]
        plane_sum = plane_sum + total(i)
    gown[0:HD, :] = g.astype(bf16)
    hi = plane_sum.astype(bf16)
    rest = plane_sum - hi.astype(f32)
    mid = rest.astype(bf16)
    low = (rest - mid.astype(f32)).astype(bf16)
    tail_rows = lax.broadcasted_iota(jnp.int32, (16, HD // 2), 0)
    gown[HD:HD + 16, :] = jnp.where(
        tail_rows == 0, hi.astype(f32), jnp.where(tail_rows == 1, mid.astype(f32), jnp.where(tail_rows == 2, low.astype(f32), 0.0))
    ).astype(bf16)
    start_own(2)

    for kind in (2, 3):
        locals_[kind].wait()
        for r in order:
            x_copy(kind, r).wait_recv()

    def attend(kb, vb, first):
        k = kb[...]
        v = vb[...]
        for i in range(X):
            q = qbuf[i].reshape(2 * T, HD)
            at = pl.ds(i * 2 * T, 2 * T)
            s = mm(q, k, NT)
            if first:
                t_pos = lax.rem(lax.broadcasted_iota(jnp.int32, (2 * T, T), 0), T)
                ok = t_pos + (i - x) * T >= lax.broadcasted_iota(jnp.int32, (2 * T, T), 1)
                s = jnp.where(ok, s, NEG)
                m_new = jnp.broadcast_to(jnp.max(s, axis=1, keepdims=True), (2 * T, T))
                p = jnp.where(ok, jnp.exp2((s - m_new) * SCALE2), 0.0)
                l_s[at, :] = p
                acc[at, :] = mm(p.astype(bf16), v)
            else:
                m_old = m_s[at, :]
                m_new = jnp.maximum(m_old, jnp.max(s, axis=1, keepdims=True))
                p = jnp.exp2((s - m_new) * SCALE2)
                alpha = jnp.exp2((m_old - m_new) * SCALE2)
                l_s[at, :] = l_s[at, :] * alpha + p
                acc[at, :] = acc[at, :] * wide(alpha) + mm(p.astype(bf16), v)
            m_s[at, :] = m_new

    attend(own.at[0], own.at[1], True)
    s_f[...] = jnp.zeros_like(s_f)
    s_b[...] = jnp.zeros_like(s_b)
    e_f[...] = jnp.zeros_like(e_f)

    def plane_decay(way, i):
        tail = gbuf[way, i, HD:HD + 16, :].astype(f32)
        return tail[0:1, :] + tail[1:2, :] + tail[2:3, :]

    def receive(way, i, got, passed):
        for t in range(3):
            @pl.when(i < got)
            def _():
                remote(mine(t), slot(t, way, i), z_send.at[t, way, 0], z_recv.at[t, way, i], up if way == 0 else down).wait_recv()

            @pl.when(i < passed)
            def _():
                pass_on(t, way, i).start()

    def step(i, carry):
        receive(0, i, got_up, pass_up)
        receive(1, i, got_down, pass_down)

        @pl.when(i < got_up)
        def _():
            attend(kv.at[0, 0, i], kv.at[1, 0, i], False)
            s_f[...] = s_f[...] + jnp.exp(e_f[0:1, :]) * gbuf[0, i, 0:HD, :].astype(f32)
            e_f[...] = e_f[...] + plane_decay(0, i)

        @pl.when(i < use_down)
        def _():
            attend(kv.at[0, 1, i], kv.at[1, 1, i], False)
            s_b[...] = s_b[...] * jnp.exp(plane_decay(1, i)) + gbuf[1, i, 0:HD, :].astype(f32)

        return carry

    lax.fori_loop(0, F, step, 0)

    locals_[4].wait()
    for r in order:
        x_copy(4, r).wait_recv()
    state = s_f[...] + jnp.exp(e_f[0:1, :]) * s_b[...]
    for i in range(X):
        top = state.astype(bf16)
        low_part = (state - top.astype(f32)).astype(bf16)
        fb_send[i] = mm(qr[i], top) + mm(qr[i], low_part)
        if i < X - 1:
            state = state * jnp.exp(total(i)) + sum_recv[i]
    for r in order:
        x_copy(7, r).start()

    lane = lax.broadcasted_iota(jnp.int32, (T, T), 1)
    for r in order:
        xp, _ = xdev(r)
        stat = jnp.zeros((T, T), f32)
        for hh in range(2):
            at = pl.ds(pl.multiple_of((xp * 2 + hh) * T, T), T)
            l = jnp.sum(l_s[at, :], axis=1, keepdims=True)
            o_send[xp, hh] = (acc[at, :] / jnp.where(l > 0.0, l, 1.0)).astype(bf16)
            stat = jnp.where(lane == 2 * hh, m_s[at, :], stat)
            stat = jnp.where(lane == 2 * hh + 1, l, stat)
        st_send[xp] = stat.T[0:8, :]
        x_copy(6, r).start()
        x_copy(5, r).start()

    for r in order:
        x_copy(7, r).wait_recv()
    fb_recv[x] = fb_send[x]
    for hh in range(2):
        d = jnp.exp(d_s[hh])
        before = jnp.concatenate([fb_recv[2 * hh], fb_recv[2 * hh + 1]], axis=1)
        kept = within[hh] + wide(d) * before
        normed = kept * lax.rsqrt(jnp.mean(kept * kept, axis=1, keepdims=True) + EPS)
        o_ret[:, hh * HD:(hh + 1) * HD] = (normed * silu[hh]).astype(bf16)

    for kind in (6, 5):
        for r in order:
            x_copy(kind, r).wait_recv()
    stats = {}
    for r in order:
        xp, _ = xdev(r)
        stats[r] = (xp, jnp.concatenate([st_recv[xp]] * (T // 8), axis=0).T)
    for hh in range(2):
        at = pl.ds(pl.multiple_of((x * 2 + hh) * T, T), T)
        m_own = m_s[at, :][:, 0:1]
        l_own = jnp.sum(l_s[at, :], axis=1, keepdims=True)
        top = m_own
        for r in order:
            top = jnp.maximum(top, stats[r][1][:, 2 * hh:2 * hh + 1])
        w_own = jnp.exp2((m_own - top) * SCALE2)
        out = acc[at, :] * w_own
        weight = l_own * w_own
        for r in order:
            xp, st = stats[r]
            w = jnp.exp2((st[:, 2 * hh:2 * hh + 1] - top) * SCALE2) * st[:, 2 * hh + 1:2 * hh + 2]
            out = out + o_recv[xp, hh].astype(f32) * w
            weight = weight + w
        o_x[:, hh * HD:(hh + 1) * HD] = (out / weight).astype(bf16)

    for r in range(1, NH):
        for t in range(2):
            cache_copy(r, t).wait_send()
    for kind in range(8):
        for r in order:
            x_copy(kind, r).wait_send()
    for t in range(3):
        @pl.when(own_up)
        def _():
            send_own(t, 0).wait_send()

        @pl.when(own_down)
        def _():
            send_own(t, 1).wait_send()

    def drain(i, carry):
        for t in range(3):
            @pl.when(i < pass_up)
            def _():
                pass_on(t, 0, i).wait_send()

            @pl.when(i < pass_down)
            def _():
                pass_on(t, 1, i).wait_send()
        return carry

    lax.fori_loop(0, F, drain, 0)


def per_device(Z, NH, *args):
    T = args[0].shape[0]
    F = Z // 2
    W = HD // 2
    vm = pltpu.VMEM
    dma = pltpu.SemaphoreType.DMA
    out = jax.ShapeDtypeStruct((T, 2 * HD), bf16)
    return pl.pallas_call(
        functools.partial(kernel, Z, NH, T),
        out_shape=(out, out),
        in_specs=[pl.BlockSpec(memory_space=pltpu.VMEM)] * 8,
        out_specs=(pl.BlockSpec(memory_space=pltpu.VMEM),) * 2,
        scratch_shapes=[
            vm((X, 2, T, HD), bf16), vm((2, T, HD), bf16), vm((2, 2, F, T, HD), bf16),
            vm((HD + 16, W), bf16), vm((2, F, HD + 16, W), bf16),
            vm((X * 2 * T, T), f32), vm((X * 2 * T, T), f32), vm((X * 2 * T, HD), f32),
            vm((X, 2, T, HD), bf16), vm((X, 2, T, HD), bf16), vm((X, 8, T), f32), vm((X, 8, T), f32),
            vm((2, T, T), f32), vm((2, T, HD), f32), vm((2, T, HD), f32),
            vm((4, HD, W), f32), vm((X, HD, W), f32), vm((8, T), f32), vm((X, 8, T), f32),
            vm((X, T, HD), bf16), vm((HD, W), f32), vm((HD, W), f32), vm((8, T), f32),
            vm((X, T, W), f32), vm((X, T, W), f32),
            dma((5,)), dma((2, NH)), dma((2, NH)), dma((8, X)), dma((8, X)),
            dma((3, 2, F + 1)), dma((3, 2, F + 1)),
        ],
        compiler_params=pltpu.CompilerParams(collective_id=0, has_side_effects=True),
        name="block",
    )(*args)


def solution(mesh):
    Z, NH = mesh.shape["ctx"] // X, mesh.shape["head"]
    split = P("ctx", "head")
    rows = P(("ctx", "head"), None)
    return jax.shard_map(
        functools.partial(per_device, Z, NH),
        mesh=mesh,
        in_specs=(split,) * 6 + (rows,) * 2,
        out_specs=(split, split),
        check_vma=False,
    )
```

```python
import functools
import math

import jax
import jax.numpy as jnp
from jax import lax
from jax.experimental import pallas as pl
from jax.experimental.pallas import tpu as pltpu
from jax.sharding import PartitionSpec as P

HD = 256
X = 4
NEG = -1e30
EPS = 1e-06
MESH = pl.DeviceIdType.MESH
bf16, f32 = jnp.bfloat16, jnp.float32
SCALE2 = math.log2(math.e) / math.sqrt(HD)
NT = (((1,), (1,)), ((), ()))
TN = (((0,), (0,)), ((), ()))


def mm(a, b, dims=(((1,), (0,)), ((), ()))):
    return lax.dot_general(a, b, dims, preferred_element_type=f32)


def wide(a):
    return jnp.concatenate([a, a], axis=1)


def kernel(
    Z, NH, T,
    q_ret, k_ret, v_ret, gate, ld, q_x, cache_k, cache_v,
    o_ret, o_x,
    qv, kvv, vv, gv, ldv,
    qbuf, own, kv, gown, gsingle, gpair, gbuf, m_s, l_s, acc, o_send, o_recv, st_send, st_recv,
    d_s, within, silu, sum_send, sum_recv, t_send, t_recv, qr, s_f, s_b, e_f,
    fb_send, fb_recv,
    loc_sem, c_send, c_recv, x_send, x_recv, z_send, z_recv, g_send, g_recv,
):
    F = Z // 2
    B = F - 1
    RP = T // NH
    HALF = HD // 2
    c = lax.axis_index("ctx")
    h = lax.axis_index("head")
    z = lax.div(c, X)
    x = lax.rem(c, X)
    odd = lax.rem(z, 2)
    plane = z * X

    def xdev(r):
        xp = lax.rem(x + r, X)
        return xp, (plane + xp, h)

    def hdev(r):
        hp = lax.rem(h + r, NH)
        return hp, (c, hp)

    up = (lax.rem(c + X, Z * X), h)
    down = (lax.rem(c + (Z - 1) * X, Z * X), h)

    def remote(src, dst, ss, rs, dev):
        return pltpu.make_async_remote_copy(
            src_ref=src, dst_ref=dst, send_sem=ss, recv_sem=rs,
            device_id=dev, device_id_type=MESH,
        )

    barrier = pltpu.get_barrier_semaphore()
    for r in range(1, NH):
        pl.semaphore_signal(barrier, inc=1, device_id=hdev(r)[1], device_id_type=MESH)
    for r in range(1, X):
        pl.semaphore_signal(barrier, inc=1, device_id=xdev(r)[1], device_id_type=MESH)
    pl.semaphore_signal(barrier, inc=1, device_id=up, device_id_type=MESH)
    pl.semaphore_signal(barrier, inc=1, device_id=down, device_id_type=MESH)

    def head_cols(i):
        return pl.ds(pl.multiple_of(i * HD, HD), HD)

    my_rows = pl.ds(pl.multiple_of(h * RP, RP), RP)
    pairs = (
        (ld, ldv), (k_ret, kvv), (v_ret, vv),
        (cache_k.at[:, head_cols(h)], own.at[0, my_rows]),
        (cache_v.at[:, head_cols(h)], own.at[1, my_rows]),
        (q_ret, qv), (gate, gv),
        (q_x.at[:, 0:HD], qbuf.at[x, 0]),
        (q_x.at[:, HD:2 * HD], qbuf.at[x, 1]),
        (q_ret.at[:, head_cols(lax.div(x, 2))], qr.at[x]),
    )
    local = [pltpu.make_async_copy(src, dst, loc_sem.at[n]) for n, (src, dst) in enumerate(pairs)]
    for cp in local:
        cp.start()

    def cache_copy(r, t):
        src = cache_k if t == 0 else cache_v
        hp, dev = hdev(r)
        return remote(src.at[:, head_cols(hp)], own.at[t, my_rows], c_send.at[t, r], c_recv.at[t, r], dev)

    def x_copy(kind, r):
        xp, dev = xdev(r)
        if kind == 0:
            src, dst = sum_send.at[xp], sum_recv.at[x]
        elif kind == 1:
            src, dst = t_send, t_recv.at[x]
        elif kind == 2 or kind == 3:
            src, dst = q_x.at[:, (kind - 2) * HD:(kind - 1) * HD], qbuf.at[x, kind - 2]
        elif kind == 4:
            src, dst = q_ret.at[:, head_cols(lax.div(xp, 2))], qr.at[x]
        elif kind == 5:
            src, dst = o_send.at[xp], o_recv.at[x]
        elif kind == 6:
            src, dst = st_send.at[xp], st_recv.at[x]
        else:
            src, dst = fb_send.at[xp], fb_recv.at[x]
        return remote(src, dst, x_send.at[kind, r], x_recv.at[kind, r], dev)

    order = (2, 1, 3)
    pl.semaphore_wait(barrier, (NH - 1) + (X - 1) + 2)
    for t in range(2):
        for r in range(1, NH):
            cache_copy(r, t).start()
    for r in (1, 3):
        x_copy(2, r).start()
        x_copy(3, r).start()

    for n in (0, 1, 2):
        local[n].wait()
    lane8 = lax.broadcasted_iota(jnp.int32, (8, T), 1)
    for hh in range(2):
        dr = jnp.broadcast_to(ldv[hh:hh + 1, :], (8, T))
        step = 1
        while step < T:
            dr = dr + jnp.where(lane8 >= step, pltpu.roll(dr, step, 1), 0.0)
            step *= 2
        d = jnp.concatenate([dr] * (T // 8), axis=0).T
        d_s[hh] = d
        last = d[T - 1:T, :]
        fade = jnp.exp(last - d)
        kh = kvv[:, hh * HD:(hh + 1) * HD]
        vh = vv[:, hh * HD:(hh + 1) * HD]
        carried = (kh.astype(f32) * wide(fade)).astype(bf16)
        summ = mm(carried, vh, TN).astype(bf16)
        sum_send[2 * hh] = summ[:, :HALF]
        sum_send[2 * hh + 1] = summ[:, HALF:]
        t_send[4 * hh:4 * hh + 4, :] = jnp.broadcast_to(last, (4, T))
    for kind in (1, 0):
        for r in order:
            x_copy(kind, r).start()
    for kind, r in ((2, 2), (3, 2), (4, 2), (4, 1), (4, 3)):
        x_copy(kind, r).start()

    def way_dev(way):
        return up if way == 0 else down

    def send_own(t, way):
        return remote(own.at[t], kv.at[t, way, 0], z_send.at[t, way, 0], z_recv.at[t, way, 0], way_dev(way))

    low = z < F
    back_shift = jnp.where(low, 1, 0)
    back_lag = jnp.where(low, 0, Z - 1 - z)

    def pass_on(t, way, i):
        to = i + 1 if way == 0 else i + back_shift
        return remote(kv.at[t, way, i], kv.at[t, way, to], z_send.at[t, way, i + 1], z_recv.at[t, way, to], way_dev(way))

    def arrival(t, way, i):
        return remote(own.at[t], kv.at[t, way, i], z_send.at[t, way, 0], z_recv.at[t, way, i], way_dev(way))

    own_up = z < Z - 1
    own_down = z < B
    got_up = jnp.minimum(z, F)
    got_down = jnp.where(low, jnp.maximum(B - 1 - z, 0), z - F)
    use_down = jnp.where(low, 0, z - F)
    pass_up = jnp.where(own_up, jnp.minimum(z, F - 1), 0)
    pass_down = jnp.where(low, got_down, jnp.maximum(z - F - 1, 0))

    def relay(t, s):
        for way in range(2):
            i = s if way == 0 else s - back_lag
            got, passed = (got_up, pass_up) if way == 0 else (got_down, pass_down)

            @pl.when(jnp.logical_and(i >= 0, i < got))
            def _():
                arrival(t, way, i).wait_recv()

            @pl.when(jnp.logical_and(i >= 0, i < passed))
            def _():
                pass_on(t, way, i).start()

    local[3].wait()
    local[4].wait()
    for t in range(2):
        for r in range(1, NH):
            cache_copy(r, t).wait_recv()

        @pl.when(own_up)
        def _():
            send_own(t, 0).start()

        @pl.when(own_down)
        def _():
            send_own(t, 1).start()

    sum_recv[x] = sum_send[x]
    t_recv[x] = t_send[...]
    s_f[...] = jnp.zeros_like(s_f)
    s_b[...] = jnp.zeros_like(s_b)
    e_f[...] = jnp.zeros_like(e_f)
    local[5].wait()
    local[6].wait()
    rows = lax.broadcasted_iota(jnp.int32, (T, T), 0)
    cols = lax.broadcasted_iota(jnp.int32, (T, T), 1)
    for hh in range(2):
        d = d_s[hh]
        qh = qv[:, hh * HD:(hh + 1) * HD]
        kh = kvv[:, hh * HD:(hh + 1) * HD]
        vh = vv[:, hh * HD:(hh + 1) * HD]
        spread = jnp.minimum(d - d.T, 0.0)
        w = jnp.where(rows >= cols, jnp.exp(spread) * mm(qh, kh, NT), 0.0).astype(bf16)
        within[hh] = mm(w, vh)
        g = gv[:, hh * HD:(hh + 1) * HD].astype(f32)
        silu[hh] = g / (1.0 + jnp.exp(-g))

    relay(0, 0)
    relay(1, 0)

    for kind in (1, 0):
        for r in order:
            x_copy(kind, r).wait_recv()

    second = lax.div(x, 2) == 1

    def total(i):
        tr = t_recv[i]
        return jnp.where(second, tr[4:5, :], tr[0:1, :])

    tail_rows = lax.broadcasted_iota(jnp.int32, (16, HALF), 0)

    def pack(ref, value, decay):
        ref[0:HD, :] = value.astype(bf16)
        hi = decay.astype(bf16).astype(f32)
        mid = (decay - hi).astype(bf16).astype(f32)
        lowest = decay - hi - mid
        rest = jnp.where(tail_rows == 0, hi, jnp.where(tail_rows == 1, mid, jnp.where(tail_rows == 2, lowest, 0.0)))
        ref[HD:HD + 16, :] = rest.astype(bf16)

    def unpack(ref):
        tail = ref[HD:HD + 16, :].astype(f32)
        return ref[0:HD, :].astype(f32), tail[0:1, :] + tail[1:2, :] + tail[2:3, :]

    g_own = sum_recv[0].astype(f32)
    g_decay = total(0)
    for i in range(1, X):
        g_own = g_own * jnp.exp(total(i)) + sum_recv[i].astype(f32)
        g_decay = g_decay + total(i)

    single = remote(gown, gsingle, g_send.at[0, F], g_recv.at[0, F], up)

    @pl.when(odd == 0)
    def _():
        pack(gown, g_own, g_decay)
        single.start()

    def pair_own(way):
        return remote(gpair, gbuf.at[way, 0], g_send.at[way, F + 1], g_recv.at[way, 0], way_dev(way))

    def pair_pass(way, k):
        to = jnp.where(low, k + odd, k) if way == 1 else k + odd
        return remote(gbuf.at[way, k], gbuf.at[way, to], g_send.at[way, k], g_recv.at[way, to], way_dev(way))

    pair_up = jnp.logical_and(odd == 1, own_up)
    pair_down = jnp.logical_and(odd == 1, own_down)
    g_up = jnp.minimum(lax.div(z, 2), jnp.where(odd == 1, F // 2, (F + 1) // 2))
    g_down = jnp.where(low, jnp.maximum(B // 2 - lax.div(z + 1, 2), 0), lax.div(jnp.maximum(z - F, 0), 2))
    g_pass_up = jnp.where(own_up, jnp.minimum(g_up, jnp.where(odd == 1, (F - 1) // 2, F // 2)), 0)
    g_pass_down = jnp.where(low, g_down, lax.div(jnp.maximum(z - 1 - F, 0), 2))

    def pair_relay(dist):
        for way in range(2):
            if way == 0:
                off = dist - 1 - odd
                got, passed = g_up, g_pass_up
            else:
                off = dist - 1 - jnp.where(low, odd, Z - z)
                got, passed = g_down, g_pass_down
            k = lax.div(jnp.maximum(off, 0), 2)
            here = jnp.logical_and(off >= 0, lax.rem(jnp.maximum(off, 0), 2) == 0)

            @pl.when(jnp.logical_and(here, k < got))
            def _():
                remote(gpair, gbuf.at[way, k], g_send.at[way, F + 1], g_recv.at[way, k], way_dev(way)).wait_recv()

            @pl.when(jnp.logical_and(here, k < passed))
            def _():
                pair_pass(way, k).start()

            if way == 0:
                @pl.when(jnp.logical_and(here, k < got))
                def _():
                    g, decay = unpack(gbuf.at[0, k])
                    s_f[...] = s_f[...] + jnp.exp(e_f[0:1, :]) * g
                    e_f[...] = e_f[...] + decay
            else:
                @pl.when(jnp.logical_and(here, jnp.logical_and(k < got, z > F)))
                def _():
                    g, decay = unpack(gbuf.at[1, k])
                    s_b[...] = s_b[...] * jnp.exp(decay) + g

    relay(0, 1)
    relay(1, 1)

    @pl.when(odd == 1)
    def _():
        remote(gown, gsingle, g_send.at[0, F], g_recv.at[0, F], up).wait_recv()
        g_before, d_before = unpack(gsingle)
        s_f[...] = g_before
        e_f[...] = e_f[...] + d_before
        pack(gpair, g_before * jnp.exp(g_decay) + g_own, d_before + g_decay)

    @pl.when(pair_up)
    def _():
        pair_own(0).start()

    @pl.when(pair_down)
    def _():
        pair_own(1).start()

    def attend(kb, vb, first):
        k = kb[...]
        v = vb[...]
        for i in range(X):
            q = qbuf[i].reshape(2 * T, HD)
            at = pl.ds(i * 2 * T, 2 * T)
            s = mm(q, k, NT)
            if first:
                t_pos = lax.rem(lax.broadcasted_iota(jnp.int32, (2 * T, T), 0), T)
                ok = t_pos + (i - x) * T >= lax.broadcasted_iota(jnp.int32, (2 * T, T), 1)
                s = jnp.where(ok, s, NEG)
                m_new = jnp.broadcast_to(jnp.max(s, axis=1, keepdims=True), (2 * T, T))
                p = jnp.where(ok, jnp.exp2((s - m_new) * SCALE2), 0.0)
                l_s[at, :] = p
                acc[at, :] = mm(p.astype(bf16), v)
            else:
                m_old = m_s[at, :]
                m_new = jnp.maximum(m_old, jnp.max(s, axis=1, keepdims=True))
                p = jnp.exp2((s - m_new) * SCALE2)
                alpha = jnp.exp2((m_old - m_new) * SCALE2)
                l_s[at, :] = l_s[at, :] * alpha + p
                acc[at, :] = acc[at, :] * wide(alpha) + mm(p.astype(bf16), v)
            m_s[at, :] = m_new

    for n in (7, 8):
        local[n].wait()
    for kind in (2, 3):
        for r in order:
            x_copy(kind, r).wait_recv()
    attend(own.at[0], own.at[1], True)

    def attend_slots(way, lo, hi):
        def one(n, carry):
            i = n if way == 0 else n - back_lag

            @pl.when(jnp.logical_and(i >= 0, i < (got_up if way == 0 else use_down)))
            def _():
                attend(kv.at[0, way, i], kv.at[1, way, i], False)

            return carry

        lax.fori_loop(lo, hi, one, 0)

    def reach(s):
        return jnp.where(s < 2, 0, jnp.where(s == 2, 1, s))

    def step(s, carry):
        lo, hi = reach(s - 1), reach(s)
        relay(0, s)
        attend_slots(0, lo, hi)
        relay(1, s)
        attend_slots(1, lo, hi)
        pair_relay(s - 1)
        return carry

    lax.fori_loop(2, F, step, 0)

    def final(n, carry):
        for way in range(2):
            attend_slots(way, n, n + 1)
        return carry

    lax.fori_loop(reach(jnp.int32(F - 1)), F, final, 0)

    lane = lax.broadcasted_iota(jnp.int32, (T, T), 1)
    for r in order:
        xp, _ = xdev(r)
        stat = jnp.zeros((T, T), f32)
        for hh in range(2):
            at = pl.ds(pl.multiple_of((xp * 2 + hh) * T, T), T)
            l = jnp.sum(l_s[at, :], axis=1, keepdims=True)
            o_send[xp, hh] = (acc[at, :] / jnp.where(l > 0.0, l, 1.0)).astype(bf16)
            stat = jnp.where(lane == 2 * hh, m_s[at, :], stat)
            stat = jnp.where(lane == 2 * hh + 1, l, stat)
        st_send[xp] = stat.T[0:8, :]
        x_copy(6, r).start()
        x_copy(5, r).start()

    def late(dist, carry):
        pair_relay(dist)
        return carry

    lax.fori_loop(F - 1, F + 1, late, 0)

    local[9].wait()
    for r in order:
        x_copy(4, r).wait_recv()
    state = s_f[...] + jnp.exp(e_f[0:1, :]) * s_b[...]
    for i in range(X):
        top = state.astype(bf16)
        low_part = (state - top.astype(f32)).astype(bf16)
        fb_send[i] = mm(qr[i], top) + mm(qr[i], low_part)
        if i < X - 1:
            state = state * jnp.exp(total(i)) + sum_recv[i].astype(f32)
    for r in order:
        x_copy(7, r).start()

    for kind in (6, 5):
        for r in order:
            x_copy(kind, r).wait_recv()
    stats = {}
    for r in order:
        xp, _ = xdev(r)
        stats[r] = (xp, jnp.concatenate([st_recv[xp]] * (T // 8), axis=0).T)
    for hh in range(2):
        at = pl.ds(pl.multiple_of((x * 2 + hh) * T, T), T)
        m_own = m_s[at, :][:, 0:1]
        l_own = jnp.sum(l_s[at, :], axis=1, keepdims=True)
        top = m_own
        for r in order:
            top = jnp.maximum(top, stats[r][1][:, 2 * hh:2 * hh + 1])
        w_own = jnp.exp2((m_own - top) * SCALE2)
        out = acc[at, :] * w_own
        weight = l_own * w_own
        for r in order:
            xp, st = stats[r]
            w = jnp.exp2((st[:, 2 * hh:2 * hh + 1] - top) * SCALE2) * st[:, 2 * hh + 1:2 * hh + 2]
            out = out + o_recv[xp, hh].astype(f32) * w
            weight = weight + w
        o_x[:, hh * HD:(hh + 1) * HD] = (out / weight).astype(bf16)

    for r in order:
        x_copy(7, r).wait_recv()
    fb_recv[x] = fb_send[x]
    for hh in range(2):
        d = jnp.exp(d_s[hh])
        before = jnp.concatenate([fb_recv[2 * hh], fb_recv[2 * hh + 1]], axis=1)
        kept = within[hh] + wide(d) * before
        normed = kept * lax.rsqrt(jnp.mean(kept * kept, axis=1, keepdims=True) + EPS)
        o_ret[:, hh * HD:(hh + 1) * HD] = (normed * silu[hh]).astype(bf16)

    for r in range(1, NH):
        for t in range(2):
            cache_copy(r, t).wait_send()
    for kind in range(8):
        for r in order:
            x_copy(kind, r).wait_send()
    for t in range(2):
        @pl.when(own_up)
        def _():
            send_own(t, 0).wait_send()

        @pl.when(own_down)
        def _():
            send_own(t, 1).wait_send()

    @pl.when(odd == 0)
    def _():
        remote(gown, gsingle, g_send.at[0, F], g_recv.at[0, F], up).wait_send()

    @pl.when(pair_up)
    def _():
        pair_own(0).wait_send()

    @pl.when(pair_down)
    def _():
        pair_own(1).wait_send()

    def drain(i, carry):
        for way, passed, g_passed in ((0, pass_up, g_pass_up), (1, pass_down, g_pass_down)):
            for t in range(2):
                @pl.when(i < passed)
                def _():
                    pass_on(t, way, i).wait_send()

            @pl.when(i < g_passed)
            def _():
                pair_pass(way, i).wait_send()
        return carry

    lax.fori_loop(0, F, drain, 0)


def per_device(Z, NH, q_ret, k_ret, v_ret, gate, log_decay, q_x, cache_k, cache_v):
    T = q_ret.shape[0]
    F = Z // 2
    W = HD // 2
    vm = pltpu.VMEM
    dma = pltpu.SemaphoreType.DMA
    out = jax.ShapeDtypeStruct((T, 2 * HD), bf16)
    item = (HD + 16, W)
    return pl.pallas_call(
        functools.partial(kernel, Z, NH, T),
        out_shape=(out, out),
        in_specs=[pl.BlockSpec(memory_space=pl.ANY)] * 8,
        out_specs=(pl.BlockSpec(memory_space=pltpu.VMEM),) * 2,
        scratch_shapes=[
            vm((T, 2 * HD), bf16), vm((T, 2 * HD), bf16), vm((T, 2 * HD), bf16), vm((T, 2 * HD), bf16), vm((2, T), f32),
            vm((X, 2, T, HD), bf16), vm((2, T, HD), bf16), vm((2, 2, F, T, HD), bf16),
            vm(item, bf16), vm(item, bf16), vm(item, bf16), vm((2, F // 2 + 1) + item, bf16),
            vm((X * 2 * T, T), f32), vm((X * 2 * T, T), f32), vm((X * 2 * T, HD), f32),
            vm((X, 2, T, HD), bf16), vm((X, 2, T, HD), bf16), vm((X, 8, T), f32), vm((X, 8, T), f32),
            vm((2, T, T), f32), vm((2, T, HD), f32), vm((2, T, HD), f32),
            vm((4, HD, W), bf16), vm((X, HD, W), bf16), vm((8, T), f32), vm((X, 8, T), f32),
            vm((X, T, HD), bf16), vm((HD, W), f32), vm((HD, W), f32), vm((8, T), f32),
            vm((X, T, W), f32), vm((X, T, W), f32),
            dma((10,)), dma((2, NH)), dma((2, NH)), dma((8, X)), dma((8, X)),
            dma((2, 2, F + 1)), dma((2, 2, F + 1)), dma((2, F + 2)), dma((2, F + 2)),
        ],
        compiler_params=pltpu.CompilerParams(collective_id=0, has_side_effects=True),
        name="block",
    )(q_ret, k_ret, v_ret, gate, log_decay.T, q_x, cache_k, cache_v)


def solution(mesh):
    Z, NH = mesh.shape["ctx"] // X, mesh.shape["head"]
    split = P("ctx", "head")
    rows = P(("ctx", "head"), None)
    return jax.shard_map(
        functools.partial(per_device, Z, NH),
        mesh=mesh,
        in_specs=(split,) * 6 + (rows,) * 2,
        out_specs=(split, split),
        check_vma=False,
    )
```

```python
import functools
import math

import jax
import jax.numpy as jnp
from jax import lax
from jax.experimental import pallas as pl
from jax.experimental.pallas import tpu as pltpu
from jax.sharding import PartitionSpec as P

HD = 256
X = 4
NEG = -1e30
EPS = 1e-06
MESH = pl.DeviceIdType.MESH
bf16, f32 = jnp.bfloat16, jnp.float32
SCALE2 = math.log2(math.e) / math.sqrt(HD)
NT = (((1,), (1,)), ((), ()))
TN = (((0,), (0,)), ((), ()))


def mm(a, b, dims=(((1,), (0,)), ((), ()))):
    return lax.dot_general(a, b, dims, preferred_element_type=f32)


def wide(a):
    return jnp.concatenate([a, a], axis=1)


def kernel(
    Z, NH, T,
    q_ret, k_ret, v_ret, gate, ld, q_x, cache_k, cache_v,
    o_ret, o_x,
    qv, kvv, vv, gv, ldv, cv, ox_v, or_v,
    qbuf, own, kv, gown, gsingle, gpair, gbuf, m_s, l_s, acc, o_send, o_recv, st_send, st_recv,
    d_s, within, silu, sum_send, sum_recv, t_send, t_recv, qr, s_f, s_b, e_f,
    fb_send, fb_recv,
    loc_sem, c_send, c_recv, x_send, x_recv, z_send, z_recv, g_send, g_recv,
):
    F = Z // 2 - 1
    B = Z - 1 - F
    STEPS = max(F, B)
    FG = Z // 2
    BG = Z - 1 - FG
    RP = T // NH
    HALF = HD // 2
    c = lax.axis_index("ctx")
    h = lax.axis_index("head")
    z = lax.div(c, X)
    x = lax.rem(c, X)
    odd = lax.rem(z, 2)
    plane = z * X

    def xdev(r):
        xp = lax.rem(x + r, X)
        return xp, (plane + xp, h)

    def hdev(r):
        hp = lax.rem(h + r, NH)
        return hp, (c, hp)

    up = (lax.rem(c + X, Z * X), h)
    down = (lax.rem(c + (Z - 1) * X, Z * X), h)

    def remote(src, dst, ss, rs, dev):
        return pltpu.make_async_remote_copy(
            src_ref=src, dst_ref=dst, send_sem=ss, recv_sem=rs,
            device_id=dev, device_id_type=MESH,
        )

    barrier = pltpu.get_barrier_semaphore()
    for r in range(1, NH):
        pl.semaphore_signal(barrier, inc=1, device_id=hdev(r)[1], device_id_type=MESH)
    for r in range(1, X):
        pl.semaphore_signal(barrier, inc=1, device_id=xdev(r)[1], device_id_type=MESH)
    pl.semaphore_signal(barrier, inc=1, device_id=up, device_id_type=MESH)
    pl.semaphore_signal(barrier, inc=1, device_id=down, device_id_type=MESH)

    def head_cols(i):
        return pl.ds(pl.multiple_of(i * HD, HD), HD)

    my_rows = pl.ds(pl.multiple_of(h * RP, RP), RP)
    pairs = (
        (ld, ldv), (k_ret, kvv), (v_ret, vv),
        (cache_k, cv.at[0]), (cache_v, cv.at[1]),
        (q_x.at[:, 0:HD], qbuf.at[x, 0]),
        (q_x.at[:, HD:2 * HD], qbuf.at[x, 1]),
        (cache_k.at[:, head_cols(h)], own.at[0, my_rows]),
        (cache_v.at[:, head_cols(h)], own.at[1, my_rows]),
        (q_ret, qv), (gate, gv),
        (q_ret.at[:, head_cols(lax.div(x, 2))], qr.at[x]),
    )
    local = [pltpu.make_async_copy(src, dst, loc_sem.at[n]) for n, (src, dst) in enumerate(pairs)]
    for n in (3, 4, 0, 1, 2, 5, 6, 7, 8, 9, 10, 11):
        local[n].start()

    def cache_copy(r, t):
        hp, dev = hdev(r)
        return remote(cv.at[t, :, head_cols(hp)], own.at[t, my_rows], c_send.at[t, r], c_recv.at[t, r], dev)

    def x_copy(kind, r):
        xp, dev = xdev(r)
        if kind == 0:
            src, dst = sum_send.at[xp], sum_recv.at[x]
        elif kind == 1:
            src, dst = t_send, t_recv.at[x]
        elif kind == 2 or kind == 3:
            src, dst = qbuf.at[x, kind - 2], qbuf.at[x, kind - 2]
        elif kind == 4:
            src, dst = q_ret.at[:, head_cols(lax.div(xp, 2))], qr.at[x]
        elif kind == 5:
            src, dst = o_send.at[xp], o_recv.at[x]
        elif kind == 6:
            src, dst = st_send.at[xp], st_recv.at[x]
        else:
            src, dst = fb_send.at[xp], fb_recv.at[x]
        return remote(src, dst, x_send.at[kind, r], x_recv.at[kind, r], dev)

    order = (2, 1, 3)
    for n in (3, 4):
        local[n].wait()
    pl.semaphore_wait(barrier, (NH - 1) + (X - 1) + 2)
    for t in range(2):
        for r in range(1, NH):
            cache_copy(r, t).start()

    for n in (0, 1, 2):
        local[n].wait()
    lane8 = lax.broadcasted_iota(jnp.int32, (8, T), 1)
    for hh in range(2):
        dr = jnp.broadcast_to(ldv[hh:hh + 1, :], (8, T))
        step = 1
        while step < T:
            dr = dr + jnp.where(lane8 >= step, pltpu.roll(dr, step, 1), 0.0)
            step *= 2
        d = jnp.concatenate([dr] * (T // 8), axis=0).T
        d_s[hh] = d
        last = d[T - 1:T, :]
        fade = jnp.exp(last - d)
        kh = kvv[:, hh * HD:(hh + 1) * HD]
        vh = vv[:, hh * HD:(hh + 1) * HD]
        carried = (kh.astype(f32) * wide(fade)).astype(bf16)
        summ = mm(carried, vh, TN).astype(bf16)
        sum_send[2 * hh] = summ[:, :HALF]
        sum_send[2 * hh + 1] = summ[:, HALF:]
        t_send[4 * hh:4 * hh + 4, :] = jnp.broadcast_to(last, (4, T))
    for kind in (1, 0):
        for r in order:
            x_copy(kind, r).start()
    for n in (5, 6):
        local[n].wait()
    for kind in (2, 3, 4):
        for r in order:
            x_copy(kind, r).start()

    def way_dev(way):
        return up if way == 0 else down

    PT = T // 2

    def piece(t):
        return t // 2, pl.ds((t % 2) * PT, PT)

    def mine(t):
        return own.at[piece(t)[0], piece(t)[1]]

    def slot(t, way, i):
        return kv.at[piece(t)[0], way, i, piece(t)[1]]

    def send_own(t, way):
        return remote(mine(t), slot(t, way, 0), z_send.at[t, way, 0], z_recv.at[t, way, 0], way_dev(way))

    low = z < STEPS
    back_shift = jnp.where(low, 1, 0)
    back_lag = jnp.where(low, 0, Z - 1 - z)

    def pass_on(t, way, i):
        to = i + 1 if way == 0 else i + back_shift
        return remote(slot(t, way, i), slot(t, way, to), z_send.at[t, way, i + 1], z_recv.at[t, way, to], way_dev(way))

    def arrival(t, way, i):
        return remote(mine(t), slot(t, way, i), z_send.at[t, way, 0], z_recv.at[t, way, i], way_dev(way))

    own_up = z < Z - 1
    own_down = z < B
    got_up = jnp.minimum(z, F)
    got_down = jnp.where(low, jnp.maximum(B - 1 - z, 0), jnp.maximum(z - F, 0))
    use_down = jnp.where(low, 0, jnp.maximum(z - F, 0))
    pass_up = jnp.where(own_up, jnp.minimum(z, F - 1), 0)
    pass_down = jnp.where(low, got_down, jnp.maximum(z - F - 1, 0))

    def relay(t, s):
        for way in range(2):
            i = s if way == 0 else s - back_lag
            got, passed = (got_up, pass_up) if way == 0 else (got_down, pass_down)

            @pl.when(jnp.logical_and(i >= 0, i < got))
            def _():
                arrival(t, way, i).wait_recv()

            @pl.when(jnp.logical_and(i >= 0, i < passed))
            def _():
                pass_on(t, way, i).start()

    def start_own(t):
        local[7 + t].wait()
        for r in range(1, NH):
            cache_copy(r, t).wait_recv()
        for p in (2 * t, 2 * t + 1):
            @pl.when(own_up)
            def _():
                send_own(p, 0).start()

            @pl.when(own_down)
            def _():
                send_own(p, 1).start()

    start_own(0)

    sum_recv[x] = sum_send[x]
    t_recv[x] = t_send[...]
    s_f[...] = jnp.zeros_like(s_f)
    s_b[...] = jnp.zeros_like(s_b)
    e_f[...] = jnp.zeros_like(e_f)
    def local_part():
        local[9].wait()
        local[10].wait()
        rows = lax.broadcasted_iota(jnp.int32, (T, T), 0)
        cols = lax.broadcasted_iota(jnp.int32, (T, T), 1)
        for hh in range(2):
            d = d_s[hh]
            qh = qv[:, hh * HD:(hh + 1) * HD]
            kh = kvv[:, hh * HD:(hh + 1) * HD]
            vh = vv[:, hh * HD:(hh + 1) * HD]
            spread = jnp.minimum(d - d.T, 0.0)
            w = jnp.where(rows >= cols, jnp.exp(spread) * mm(qh, kh, NT), 0.0).astype(bf16)
            within[hh] = mm(w, vh)
            g = gv[:, hh * HD:(hh + 1) * HD].astype(f32)
            silu[hh] = g / (1.0 + jnp.exp(-g))

    def attend(kb, vb, first):
        k = kb[...]
        v = vb[...]
        for i in range(X):
            q = qbuf[i].reshape(2 * T, HD)
            at = pl.ds(i * 2 * T, 2 * T)
            s = mm(q, k, NT)
            if first:
                t_pos = lax.rem(lax.broadcasted_iota(jnp.int32, (2 * T, T), 0), T)
                ok = t_pos + (i - x) * T >= lax.broadcasted_iota(jnp.int32, (2 * T, T), 1)
                s = jnp.where(ok, s, NEG)
                m_new = jnp.broadcast_to(jnp.max(s, axis=1, keepdims=True), (2 * T, T))
                p = jnp.where(ok, jnp.exp2((s - m_new) * SCALE2), 0.0)
                l_s[at, :] = p
                acc[at, :] = mm(p.astype(bf16), v)
            else:
                m_old = m_s[at, :]
                m_new = jnp.maximum(m_old, jnp.max(s, axis=1, keepdims=True))
                p = jnp.exp2((s - m_new) * SCALE2)
                alpha = jnp.exp2((m_old - m_new) * SCALE2)
                l_s[at, :] = l_s[at, :] * alpha + p
                acc[at, :] = acc[at, :] * wide(alpha) + mm(p.astype(bf16), v)
            m_s[at, :] = m_new

    def attend_slot(way, n):
        i = n if way == 0 else n - back_lag

        @pl.when(jnp.logical_and(i >= 0, i < (got_up if way == 0 else use_down)))
        def _():
            attend(kv.at[0, way, i], kv.at[1, way, i], False)


    for kind in (1, 0):
        for r in order:
            x_copy(kind, r).wait_recv()

    second = lax.div(x, 2) == 1

    def total(i):
        tr = t_recv[i]
        return jnp.where(second, tr[4:5, :], tr[0:1, :])

    tail_rows = lax.broadcasted_iota(jnp.int32, (16, HALF), 0)

    def pack(ref, value, decay):
        ref[0:HD, :] = value.astype(bf16)
        hi = decay.astype(bf16).astype(f32)
        mid = (decay - hi).astype(bf16).astype(f32)
        lowest = decay - hi - mid
        rest = jnp.where(tail_rows == 0, hi, jnp.where(tail_rows == 1, mid, jnp.where(tail_rows == 2, lowest, 0.0)))
        ref[HD:HD + 16, :] = rest.astype(bf16)

    def unpack(ref):
        tail = ref[HD:HD + 16, :].astype(f32)
        return ref[0:HD, :].astype(f32), tail[0:1, :] + tail[1:2, :] + tail[2:3, :]

    g_own = sum_recv[0].astype(f32)
    g_decay = total(0)
    for i in range(1, X):
        g_own = g_own * jnp.exp(total(i)) + sum_recv[i].astype(f32)
        g_decay = g_decay + total(i)

    cut = (pl.ds(0, HALF), pl.ds(HALF, HALF + 16))

    def single(p):
        return remote(gown.at[cut[p]], gsingle.at[cut[p]], g_send.at[p, 0, FG], g_recv.at[p, 0, FG], up)

    @pl.when(odd == 0)
    def _():
        pack(gown, g_own, g_decay)
        for p in range(2):
            single(p).start()

    start_own(1)

    def pair_own(way, p):
        return remote(gpair.at[cut[p]], gbuf.at[way, 0, cut[p]], g_send.at[p, way, FG + 1], g_recv.at[p, way, 0], way_dev(way))

    def pair_pass(way, k, p):
        to = jnp.where(low, k + odd, k) if way == 1 else k + odd
        return remote(gbuf.at[way, k, cut[p]], gbuf.at[way, to, cut[p]], g_send.at[p, way, k], g_recv.at[p, way, to], way_dev(way))

    pair_up = jnp.logical_and(odd == 1, own_up)
    pair_down = jnp.logical_and(odd == 1, z < BG)
    g_up = jnp.minimum(lax.div(z, 2), jnp.where(odd == 1, FG // 2, (FG + 1) // 2))
    g_down = jnp.where(low, jnp.maximum(BG // 2 - lax.div(z + 1, 2), 0), lax.div(jnp.maximum(z - FG, 0), 2))
    g_pass_up = jnp.where(own_up, jnp.minimum(g_up, jnp.where(odd == 1, (FG - 1) // 2, FG // 2)), 0)
    g_pass_down = jnp.where(low, g_down, lax.div(jnp.maximum(z - 1 - FG, 0), 2))

    def pair_relay(dist):
        for way in range(2):
            if way == 0:
                off = dist - 1 - odd
                got, passed = g_up, g_pass_up
            else:
                off = dist - 1 - jnp.where(low, odd, Z - z)
                got, passed = g_down, g_pass_down
            k = lax.div(jnp.maximum(off, 0), 2)
            here = jnp.logical_and(off >= 0, lax.rem(jnp.maximum(off, 0), 2) == 0)

            for p in range(2):
                @pl.when(jnp.logical_and(here, k < got))
                def _():
                    remote(gpair.at[cut[p]], gbuf.at[way, k, cut[p]], g_send.at[p, way, FG + 1], g_recv.at[p, way, k], way_dev(way)).wait_recv()

                @pl.when(jnp.logical_and(here, k < passed))
                def _():
                    pair_pass(way, k, p).start()

            if way == 0:
                @pl.when(jnp.logical_and(here, k < got))
                def _():
                    g, decay = unpack(gbuf.at[0, k])
                    s_f[...] = s_f[...] + jnp.exp(e_f[0:1, :]) * g
                    e_f[...] = e_f[...] + decay
            else:
                @pl.when(jnp.logical_and(here, jnp.logical_and(k < got, z > FG)))
                def _():
                    g, decay = unpack(gbuf.at[1, k])
                    s_b[...] = s_b[...] * jnp.exp(decay) + g

    relay(0, 0)
    relay(1, 0)

    @pl.when(odd == 1)
    def _():
        for p in range(2):
            single(p).wait_recv()
        g_before, d_before = unpack(gsingle)
        s_f[...] = g_before
        e_f[...] = e_f[...] + d_before
        pack(gpair, g_before * jnp.exp(g_decay) + g_own, d_before + g_decay)

    @pl.when(pair_up)
    def _():
        for p in range(2):
            pair_own(0, p).start()

    @pl.when(pair_down)
    def _():
        for p in range(2):
            pair_own(1, p).start()

    relay(2, 0)
    relay(3, 0)
    for t in range(4):
        relay(t, 1)
    for kind in (2, 3):
        for r in order:
            x_copy(kind, r).wait_recv()
    attend(own.at[0], own.at[1], True)

    def reach(s):
        return jnp.where(s < 2, 0, jnp.where(s == 2, 1, s))

    def attend_slots(way, lo, hi):
        def one(n, carry):
            attend_slot(way, n)
            return carry

        lax.fori_loop(lo, hi, one, 0)

    def step(s, carry):
        lo, hi = reach(s - 1), reach(s)
        relay(0, s)
        relay(1, s)
        pair_relay(s - 1)
        attend_slots(0, lo, hi)
        relay(2, s)
        relay(3, s)
        attend_slots(1, lo, hi)
        return carry

    lax.fori_loop(2, STEPS, step, 0)
    for way in range(2):
        attend_slots(way, reach(jnp.int32(STEPS - 1)), STEPS)

    lane = lax.broadcasted_iota(jnp.int32, (T, T), 1)
    for r in order:
        xp, _ = xdev(r)
        stat = jnp.zeros((T, T), f32)
        for hh in range(2):
            at = pl.ds(pl.multiple_of((xp * 2 + hh) * T, T), T)
            l = jnp.sum(l_s[at, :], axis=1, keepdims=True)
            o_send[xp, hh] = (acc[at, :] * (1.0 / jnp.where(l > 0.0, l, 1.0))).astype(bf16)
            stat = jnp.where(lane == 2 * hh, m_s[at, :], stat)
            stat = jnp.where(lane == 2 * hh + 1, l, stat)
        st_send[xp] = stat.T[0:8, :]
        x_copy(6, r).start()
        x_copy(5, r).start()

    for dist in range(STEPS - 1, FG + 1):
        pair_relay(jnp.int32(dist))

    local[11].wait()
    for r in order:
        x_copy(4, r).wait_recv()
    state = s_f[...] + jnp.exp(e_f[0:1, :]) * s_b[...]
    for i in range(X):
        top = state.astype(bf16)
        low_part = (state - top.astype(f32)).astype(bf16)
        fb_send[i] = (mm(qr[i], top) + mm(qr[i], low_part)).astype(bf16)
        if i < X - 1:
            state = state * jnp.exp(total(i)) + sum_recv[i].astype(f32)
    for r in order:
        x_copy(7, r).start()

    local_part()

    stats = {}
    for r in order:
        x_copy(6, r).wait_recv()
        xp, _ = xdev(X - r)
        stats[r] = (xp, jnp.concatenate([st_recv[xp]] * (T // 8), axis=0).T)
    joined = []
    for hh in range(2):
        at = pl.ds(pl.multiple_of((x * 2 + hh) * T, T), T)
        m_own = m_s[at, :][:, 0:1]
        l_own = jnp.sum(l_s[at, :], axis=1, keepdims=True)
        top = m_own
        for r in order:
            top = jnp.maximum(top, stats[r][1][:, 2 * hh:2 * hh + 1])
        w_own = jnp.exp2((m_own - top) * SCALE2)
        weight = l_own * w_own
        shares = {}
        for r in order:
            st = stats[r][1]
            shares[r] = jnp.exp2((st[:, 2 * hh:2 * hh + 1] - top) * SCALE2) * st[:, 2 * hh + 1:2 * hh + 2]
            weight = weight + shares[r]
        inv = 1.0 / weight
        joined.append((at, w_own * inv, {r: shares[r] * inv for r in order}))
    outs = [acc[at, :] * w_own for at, w_own, _ in joined]
    for r in (1, 3, 2):
        x_copy(5, r).wait_recv()
        xp = stats[r][0]
        for hh in range(2):
            outs[hh] = outs[hh] + o_recv[xp, hh].astype(f32) * joined[hh][2][r]
    for hh in range(2):
        ox_v[:, hh * HD:(hh + 1) * HD] = outs[hh].astype(bf16)
    out_copies = [pltpu.make_async_copy(ox_v, o_x, loc_sem.at[12]), pltpu.make_async_copy(or_v, o_ret, loc_sem.at[13])]
    out_copies[0].start()

    for r in order:
        x_copy(7, r).wait_recv()
    fb_recv[x] = fb_send[x]
    for hh in range(2):
        d = jnp.exp(d_s[hh])
        before = jnp.concatenate([fb_recv[2 * hh], fb_recv[2 * hh + 1]], axis=1).astype(f32)
        kept = within[hh] + wide(d) * before
        normed = kept * lax.rsqrt(jnp.mean(kept * kept, axis=1, keepdims=True) + EPS)
        or_v[:, hh * HD:(hh + 1) * HD] = (normed * silu[hh]).astype(bf16)
    out_copies[1].start()

    for r in range(1, NH):
        for t in range(2):
            cache_copy(r, t).wait_send()
    for kind in range(8):
        for r in order:
            x_copy(kind, r).wait_send()
    for t in range(4):
        @pl.when(own_up)
        def _():
            send_own(t, 0).wait_send()

        @pl.when(own_down)
        def _():
            send_own(t, 1).wait_send()

    @pl.when(odd == 0)
    def _():
        for p in range(2):
            single(p).wait_send()

    @pl.when(pair_up)
    def _():
        for p in range(2):
            pair_own(0, p).wait_send()

    @pl.when(pair_down)
    def _():
        for p in range(2):
            pair_own(1, p).wait_send()

    def drain(i, carry):
        for way, passed, g_passed in ((0, pass_up, g_pass_up), (1, pass_down, g_pass_down)):
            for t in range(4):
                @pl.when(i < passed)
                def _():
                    pass_on(t, way, i).wait_send()

            @pl.when(i < g_passed)
            def _():
                for p in range(2):
                    pair_pass(way, i, p).wait_send()
        return carry

    lax.fori_loop(0, STEPS, drain, 0)
    for cp in out_copies:
        cp.wait()


def per_device(Z, NH, q_ret, k_ret, v_ret, gate, log_decay, q_x, cache_k, cache_v):
    T = q_ret.shape[0]
    F = Z // 2
    W = HD // 2
    vm = pltpu.VMEM
    dma = pltpu.SemaphoreType.DMA
    out = jax.ShapeDtypeStruct((T, 2 * HD), bf16)
    item = (HD + 16, W)
    return pl.pallas_call(
        functools.partial(kernel, Z, NH, T),
        out_shape=(out, out),
        in_specs=[pl.BlockSpec(memory_space=pl.ANY)] * 8,
        out_specs=(pl.BlockSpec(memory_space=pl.ANY),) * 2,
        scratch_shapes=[
            vm((T, 2 * HD), bf16), vm((T, 2 * HD), bf16), vm((T, 2 * HD), bf16), vm((T, 2 * HD), bf16), vm((2, T), f32), vm((2, T // NH, NH * HD), bf16),
            vm((T, 2 * HD), bf16), vm((T, 2 * HD), bf16),
            vm((X, 2, T, HD), bf16), vm((2, T, HD), bf16), vm((2, 2, F, T, HD), bf16),
            vm(item, bf16), vm(item, bf16), vm(item, bf16), vm((2, F // 2 + 1) + item, bf16),
            vm((X * 2 * T, T), f32), vm((X * 2 * T, T), f32), vm((X * 2 * T, HD), f32),
            vm((X, 2, T, HD), bf16), vm((X, 2, T, HD), bf16), vm((X, 8, T), f32), vm((X, 8, T), f32),
            vm((2, T, T), f32), vm((2, T, HD), f32), vm((2, T, HD), f32),
            vm((4, HD, W), bf16), vm((X, HD, W), bf16), vm((8, T), f32), vm((X, 8, T), f32),
            vm((X, T, HD), bf16), vm((HD, W), f32), vm((HD, W), f32), vm((8, T), f32),
            vm((X, T, W), bf16), vm((X, T, W), bf16),
            dma((14,)), dma((2, NH)), dma((2, NH)), dma((8, X)), dma((8, X)),
            dma((4, 2, F + 1)), dma((4, 2, F + 1)), dma((2, 2, F + 2)), dma((2, 2, F + 2)),
        ],
        compiler_params=pltpu.CompilerParams(collective_id=0, has_side_effects=True),
        name="block",
    )(q_ret, k_ret, v_ret, gate, log_decay.T, q_x, cache_k, cache_v)


def solution(mesh):
    Z, NH = mesh.shape["ctx"] // X, mesh.shape["head"]
    split = P("ctx", "head")
    rows = P(("ctx", "head"), None)
    return jax.shard_map(
        functools.partial(per_device, Z, NH),
        mesh=mesh,
        in_specs=(split,) * 6 + (rows,) * 2,
        out_specs=(split, split),
        check_vma=False,
    )
```
